32 devices in a mesh: batch: 2 (over y), replica: 4 (over x, core), proto: 4 (over z).
Axes of the slice: x: 2, y: 2, z: 4, core: 2. Of those that a mesh axis runs over, the one named last changes fastest.
Arguments:
- view_one: bfloat16 [4096, 512], P(('batch', 'replica')), may hold values from -4 to 4
- view_two: bfloat16 [4096, 512], P(('batch', 'replica')), may hold values from -4 to 4
- prototypes: bfloat16 [16384, 512], P('proto'), may hold values from -8 to 8
- pairing: int32 [8, 512], P(('batch', 'replica')), may hold values from 0 to 511, as said below
Outputs:
- grad_one: float32 [4096, 512], P(('batch', 'replica'))
- grad_two: float32 [4096, 512], P(('batch', 'replica'))
- grad_prototypes: float32 [16384, 512], P('proto')
The draws below stay inside these ranges and needn't reach their ends.
Inputs may be any that keep to these rules, and one draw needn't show every extreme that they name: Each row of pairing names every one of 0 to 511 once.
All inputs are finite; a program needn't handle non-finite values.
Results may differ from the reference program's by a relative error of at most 0.0018.
The reference program's roundings to bfloat16 on the way count: a program that leaves them out, or rounds other values in their place, can miss the bound.
Values sent between devices are 32-bit elements; how exact they have to be, the bound alone decides.
No kernel may reach another device: no remote copies, remote signals or barrier semaphores. Data moves between devices by JAX's collectives and lax.ppermute only.
A program may use at most 128 MiB of HBM per device.

```python
import math
import jax
import jax.numpy as jnp
from jax import lax

D = 512
PROTOS = 16384
ROWS = 512
ITERS = 3
SEG = 4096


def unit_direction(values):
    return values / jnp.sqrt(jnp.sum(values * values, -1, keepdims=True))


def shared_layout(key):
    base_key = jax.random.fold_in(key, 4099)
    draw_keys = jax.random.split(base_key, 5)
    speakers = max(PROTOS // 8, 4)
    centres = unit_direction(jax.random.normal(draw_keys[0], (speakers, D), jnp.float32))
    reach_top = jax.random.randint(draw_keys[1], (SEG,), 1, speakers + 1, dtype=jnp.int32)
    voices = jax.random.randint(draw_keys[2], (SEG,), 0, reach_top, dtype=jnp.int32)
    slot_ids = jax.random.permutation(draw_keys[3], PROTOS)[:speakers].astype(jnp.int32)
    blocks = SEG // ROWS
    block_keys = jax.random.split(draw_keys[4], blocks)
    pairing = jax.vmap(lambda k: jax.random.permutation(k, ROWS))(block_keys).astype(jnp.int32)
    return (centres, voices, slot_ids, pairing)


def embed_rows(centres, voices, noise, along, lengths):
    direction = along * centres[voices] + math.sqrt(1.0 - along * along) * unit_direction(noise)
    return (unit_direction(direction) * lengths).astype(jnp.bfloat16)


def draw_pairing(key, part):
    return shared_layout(key)[3]


def draw_view_one(key, part):
    centres, voices, slot_ids, pairing = shared_layout(key)
    noise_key, length_key = jax.random.split(jax.random.fold_in(key, 11))
    noise = jax.random.normal(noise_key, (SEG, D), jnp.float32)
    lengths = jnp.exp(jax.random.uniform(length_key, (SEG, 1), jnp.float32, math.log(0.5), math.log(2.0)))
    along = 0.75
    return embed_rows(centres, voices, noise, along, lengths)


def draw_view_two(key, part):
    centres, voices, slot_ids, pairing = shared_layout(key)
    blocks = SEG // ROWS
    flat = (jnp.arange(blocks, dtype=jnp.int32)[:, None] * ROWS + pairing).reshape(-1).astype(jnp.int32)
    voices_two = jnp.zeros((SEG,), jnp.int32).at[flat].set(voices)
    noise_key, length_key = jax.random.split(jax.random.fold_in(key, 12))
    noise = jax.random.normal(noise_key, (SEG, D), jnp.float32)
    lengths = jnp.exp(jax.random.uniform(length_key, (SEG, 1), jnp.float32, math.log(0.5), math.log(2.0)))
    along = 0.75
    return embed_rows(centres, voices_two, noise, along, lengths)


def draw_prototypes(key, part):
    centres, voices, slot_ids, pairing = shared_layout(key)
    noise_key, length_key = jax.random.split(jax.random.fold_in(key, 31))
    noise = jax.random.normal(noise_key, (PROTOS, D), jnp.float32)
    lengths = jnp.exp(jax.random.uniform(length_key, (PROTOS, 1), jnp.float32, math.log(1.0), math.log(4.0)))
    along = 0.9
    free_dirs = unit_direction(noise)
    placed = unit_direction(along * centres + math.sqrt(1.0 - along * along) * free_dirs[slot_ids])
    direction = free_dirs.at[slot_ids].set(placed)
    return (direction * lengths).astype(jnp.bfloat16)


def setup_inputs(seed: int = 0) -> dict:
    key_of = jax.random.split(jax.random.key(seed), 5)
    return {
        "view_one": draw_view_one(jax.random.fold_in(key_of[4], 71), 0),
        "view_two": draw_view_two(jax.random.fold_in(key_of[4], 71), 0),
        "prototypes": draw_prototypes(jax.random.fold_in(key_of[4], 71), 0),
        "pairing": draw_pairing(jax.random.fold_in(key_of[4], 71), 0),
    }


sink_eps = 0.05
softness_divisor = 0.1

def unit_rows(x):
    xf = x.astype(jnp.float32)
    inv = lax.rsqrt(lax.optimization_barrier(jnp.sum(xf * xf, -1, keepdims=True)) + 1e-06)
    return (xf * inv, inv)

def unit_back(grad, unit, inv):
    return inv * (grad - unit * lax.optimization_barrier(jnp.sum(unit * grad, -1, keepdims=True)))

def balance(similarity_logits):
    codes = jnp.exp(similarity_logits / sink_eps)
    for step in range(ITERS):
        codes = codes / lax.optimization_barrier(jnp.sum(codes, 0, keepdims=True))
        codes = codes / lax.optimization_barrier(jnp.sum(codes, 1, keepdims=True))
    return codes

def predict(similarity_logits):
    exponent_terms = jnp.exp(similarity_logits / softness_divisor)
    return exponent_terms / lax.optimization_barrier(jnp.sum(exponent_terms, 1, keepdims=True))

def reference(view_one, view_two, prototypes, pairing):
    unit_one, inv_one = unit_rows(view_one)
    unit_two, inv_two = unit_rows(view_two)
    unit_proto, inv_proto = unit_rows(prototypes)
    low_one = unit_one.astype(jnp.bfloat16)
    low_two = unit_two.astype(jnp.bfloat16)
    low_proto = unit_proto.astype(jnp.bfloat16)
    dims = (((1,), (1,)), ((), ()))
    logits_first_view = lax.dot_general(low_one, low_proto, dims, preferred_element_type=jnp.float32)
    logits_second_view = lax.dot_general(low_two, low_proto, dims, preferred_element_type=jnp.float32)
    codes_one = balance(logits_first_view)
    codes_two = balance(logits_second_view)
    blocks = pairing.shape[0]
    flat = (jnp.arange(blocks, dtype=jnp.int32)[:, None] * ROWS + pairing).reshape(-1).astype(jnp.int32)
    inverse = jnp.zeros((SEG,), jnp.int32).at[flat].set(jnp.arange(SEG, dtype=jnp.int32))
    target_one = codes_two[flat]
    target_two = codes_one[inverse]
    gradient_scale_factor = 0.5 / softness_divisor
    dscore_one = (gradient_scale_factor * (predict(logits_first_view) - target_one)).astype(jnp.bfloat16)
    dscore_two = (gradient_scale_factor * (predict(logits_second_view) - target_two)).astype(jnp.bfloat16)
    dunit_one = jnp.dot(dscore_one, low_proto, preferred_element_type=jnp.float32)
    dunit_two = jnp.dot(dscore_two, low_proto, preferred_element_type=jnp.float32)
    tdims = (((0,), (0,)), ((), ()))
    dunit_proto = lax.dot_general(dscore_one, low_one, tdims, preferred_element_type=jnp.float32)
    dunit_proto = dunit_proto + lax.dot_general(dscore_two, low_two, tdims, preferred_element_type=jnp.float32)
    grad_one = unit_back(dunit_one, unit_one, inv_one)
    grad_two = unit_back(dunit_two, unit_two, inv_two)
    grad_prototypes = unit_back(dunit_proto, unit_proto, inv_proto)
    return (grad_one, grad_two, grad_prototypes)
```

```python
import functools

import jax
import jax.numpy as jnp
from jax import lax
from jax.experimental import pallas as pl
from jax.experimental.pallas import tpu as pltpu
from jax.sharding import PartitionSpec as P

ITERS = 3
SEG_AXES = ("batch", "replica")
F32 = jnp.float32
BF16 = jnp.bfloat16

sink_eps = 0.05
softness_divisor = 0.1
LANES = 128


def params(limit_mib, axes=1):
    return pltpu.CompilerParams(
        vmem_limit_bytes=limit_mib << 20, dimension_semantics=("arbitrary",) * axes
    )


def whole(shape):
    return pl.BlockSpec(shape, lambda *_: (0,) * len(shape))


def inverse_norm(xf):
    return lax.rsqrt(jnp.sum(xf * xf, -1, keepdims=True) + 1e-06)


def unit_low(x):
    xf = x.astype(F32)
    return (xf * inverse_norm(xf)).astype(BF16)


def lane_fold(x):
    return sum(x[:, i : i + LANES] for i in range(0, x.shape[1], LANES))


def row_fold(x):
    return sum(x[i : i + 8] for i in range(0, x.shape[0], 8))


def to_row(acc):
    return jnp.sum(acc.T, axis=0, keepdims=True)


def to_column(row):
    return jnp.broadcast_to(row, (LANES, row.shape[1])).T


def total(refs, lo, hi):
    return sum(r[lo:hi, :] for r in refs)


def front_kernel(pair_ref, one_ref, two_ref, p_ref, e_ref, lowp_ref, low_ref, c_ref, t_ref, tacc):
    k = pl.program_id(0)
    rows = one_ref.shape[0]

    @pl.when(k == 0)
    def _():
        low_ref[:rows] = unit_low(one_ref[...])
        low_two = unit_low(two_ref[...])
        spread = (lax.broadcasted_iota(jnp.int32, (rows, rows), 0) == pair_ref[...]).astype(F32)
        low_ref[rows:] = jnp.dot(
            spread.T.astype(BF16), low_two, preferred_element_type=F32
        ).astype(BF16)
        tacc[...] = jnp.zeros_like(tacc)

    low_p = unit_low(p_ref[...])
    lowp_ref[...] = low_p
    step = min(rows, 64)
    for v in range(2):
        s = lax.dot_general(
            low_ref[v * rows : (v + 1) * rows],
            low_p,
            (((1,), (1,)), ((), ())),
            preferred_element_type=F32,
        )
        cacc = jnp.zeros((8, s.shape[1]), F32)
        for i in range(0, rows, step):
            e = jnp.exp(s[i : i + step] * (1.0 / softness_divisor))
            e_ref[v, i : i + step, :] = e
            tacc[v, i : i + step] += lane_fold(e)
            cacc = cacc + row_fold(e * e)
        c_ref[v : v + 1, :] = jnp.sum(cacc, axis=0, keepdims=True)

    @pl.when(k == pl.num_programs(0) - 1)
    def _():
        for v in range(2):
            t_ref[v : v + 1, :] = to_row(tacc[v])


def front(pairing, one, two, protos, width):
    rows, depth = one.shape
    count = protos.shape[0]
    return pl.pallas_call(
        front_kernel,
        grid=(count // width,),
        in_specs=[
            whole(pairing.shape),
            whole(one.shape),
            whole(two.shape),
            pl.BlockSpec((width, depth), lambda k: (k, 0)),
        ],
        out_specs=[
            pl.BlockSpec((2, rows, width), lambda k: (0, 0, k)),
            pl.BlockSpec((width, depth), lambda k: (k, 0)),
            whole((2 * rows, depth)),
            pl.BlockSpec((2, width), lambda k: (0, k)),
            whole((2, rows)),
        ],
        out_shape=[
            jax.ShapeDtypeStruct((2, rows, count), F32),
            jax.ShapeDtypeStruct((count, depth), BF16),
            jax.ShapeDtypeStruct((2 * rows, depth), BF16),
            jax.ShapeDtypeStruct((2, count), F32),
            jax.ShapeDtypeStruct((2, rows), F32),
        ],
        scratch_shapes=[pltpu.VMEM((2, rows, LANES), F32)],
        compiler_params=params(40),
        name="front",
    )(pairing, one, two, protos)


def row_kernel(n, e_ref, *refs):
    cparts, rest = refs[:n], refs[n:]
    t_refs, (out_ref, vb, acc) = rest[:-3], rest[-3:]
    k = pl.program_id(0)
    count = e_ref.shape[2]
    step = e_ref.shape[1]

    @pl.when(k == 0)
    def _():
        v = 1.0 / total(cparts, 0, 2)
        for i in range(2):
            vb[i] = jnp.broadcast_to(v[i : i + 1], (8, count))

    for i in range(2):
        a = jnp.zeros((step, LANES), F32)
        for j in range(0, count, LANES):
            e = e_ref[i, :, j : j + LANES]
            scale = jnp.concatenate([vb[i, :, j : j + LANES]] * (step // 8), axis=0)
            a = a + e * e * scale
        acc[i, pl.ds(pl.multiple_of(k * step, step), step), :] = a

    @pl.when(k == pl.num_programs(0) - 1)
    def _():
        for i in range(2):
            out_ref[i : i + 1, :] = to_row(acc[i])
        for t_ref in t_refs:
            out_ref[2:4, :] = t_ref[...]


def row_pass(e, cparts, extra=()):
    _, rows, count = e.shape
    step = min(rows, 64)
    height = 2 + 2 * len(extra)
    return pl.pallas_call(
        functools.partial(row_kernel, len(cparts)),
        grid=(rows // step,),
        in_specs=[pl.BlockSpec((2, step, count), lambda k: (0, k, 0))]
        + [whole(c.shape) for c in cparts]
        + [whole(t.shape) for t in extra],
        out_specs=whole((height, rows)),
        out_shape=jax.ShapeDtypeStruct((height, rows), F32),
        scratch_shapes=[pltpu.VMEM((2, 8, count), F32), pltpu.VMEM((2, rows, LANES), F32)],
        compiler_params=params(24),
        name="row_pass",
    )(e, *cparts, *extra)


def col_kernel(n, e_ref, *refs):
    rparts, (out_ref, ub, acc) = refs[:n], refs[n:]
    k = pl.program_id(0)
    count = e_ref.shape[2]
    step = e_ref.shape[1]

    @pl.when(k == 0)
    def _():
        u = 1.0 / total(rparts, 0, 2)
        for i in range(2):
            ub[i] = to_column(u[i : i + 1])
        acc[...] = jnp.zeros_like(acc)

    for i in range(2):
        u = ub[i, pl.ds(pl.multiple_of(k * step, step), step), :]
        for j in range(0, count, LANES):
            e = e_ref[i, :, j : j + LANES]
            acc[i, :, j : j + LANES] += row_fold(e * e * u)

    @pl.when(k == pl.num_programs(0) - 1)
    def _():
        for i in range(2):
            out_ref[i : i + 1, :] = jnp.sum(acc[i], axis=0, keepdims=True)


def col_pass(e, rparts):
    _, rows, count = e.shape
    step = min(rows, 64)
    return pl.pallas_call(
        functools.partial(col_kernel, len(rparts)),
        grid=(rows // step,),
        in_specs=[pl.BlockSpec((2, step, count), lambda k: (0, k, 0))]
        + [whole(r.shape) for r in rparts],
        out_specs=whole((2, count)),
        out_shape=jax.ShapeDtypeStruct((2, count), F32),
        scratch_shapes=[pltpu.VMEM((2, rows, LANES), F32), pltpu.VMEM((2, 8, count), F32)],
        compiler_params=params(24),
        name="col_pass",
    )(e, *rparts)


def score_kernel(nr, nc, bit_ref, e_ref, lowp_ref, pair_ref, *refs):
    tparts, rparts, cparts = refs[:nr], refs[nr : 2 * nr], refs[2 * nr : 2 * nr + nc]
    ds_ref, keep_ref, send_ref, ub, wb, acc = refs[2 * nr + nc :]
    k = pl.program_id(0)
    _, rows, width = e_ref.shape
    gain = 0.5 / softness_divisor

    @pl.when(k == 0)
    def _():
        u = gain / total(rparts, 0, 2)
        w = gain / total(tparts, 2, 4)
        for i in range(2):
            ub[i] = to_column(u[i : i + 1])
            wb[i] = to_column(w[i : i + 1])
        acc[...] = jnp.zeros_like(acc)

    v = 1.0 / total(cparts, 0, 2)
    step = min(rows, 32)
    for i in range(0, rows, step):
        for j in range(0, width, LANES):
            at = (slice(i, i + step), slice(j, j + LANES))
            e_one, e_two = e_ref[(0,) + at], e_ref[(1,) + at]
            u_one, u_two = ub[0, i : i + step], ub[1, i : i + step]
            w_one, w_two = wb[0, i : i + step], wb[1, i : i + step]
            v_one, v_two = v[0:1, j : j + LANES], v[1:2, j : j + LANES]
            d_one = e_one * w_one - e_two * e_two * u_two * v_two
            d_two = e_two * w_two - e_one * e_one * u_one * v_one
            ds_ref[i : i + step, j : j + LANES] = d_one.astype(BF16)
            ds_ref[rows + i : rows + i + step, j : j + LANES] = d_two.astype(BF16)
    acc[...] += jnp.dot(ds_ref[...], lowp_ref[...], preferred_element_type=F32)

    @pl.when(k == pl.num_programs(0) - 1)
    def _():
        spread = (lax.broadcasted_iota(jnp.int32, (rows, rows), 0) == pair_ref[...]).astype(F32)
        d_two = jnp.dot(
            spread, acc[rows:], preferred_element_type=F32, precision=lax.Precision.HIGHEST
        )

        @pl.when(bit_ref[0] == 0)
        def _():
            keep_ref[...] = acc[:rows]
            send_ref[...] = d_two

        @pl.when(bit_ref[0] != 0)
        def _():
            keep_ref[...] = d_two
            send_ref[...] = acc[:rows]


def score_grad(bit, e, low_p, pairing, tparts, rparts, cparts, width):
    _, rows, count = e.shape
    depth = low_p.shape[1]
    return pl.pallas_call(
        functools.partial(score_kernel, len(rparts), len(cparts)),
        grid_spec=pltpu.PrefetchScalarGridSpec(
            num_scalar_prefetch=1,
            grid=(count // width,),
            in_specs=[
                pl.BlockSpec((2, rows, width), lambda k, b: (0, 0, k)),
                pl.BlockSpec((width, depth), lambda k, b: (k, 0)),
                whole(pairing.shape),
            ]
            + [whole(t.shape) for t in tparts]
            + [whole(r.shape) for r in rparts]
            + [pl.BlockSpec((2, width), lambda k, b: (0, k)) for _ in cparts],
            out_specs=[
                pl.BlockSpec((2 * rows, width), lambda k, b: (0, k)),
                whole((rows, depth)),
                whole((rows, depth)),
            ],
            scratch_shapes=[
                pltpu.VMEM((2, rows, LANES), F32),
                pltpu.VMEM((2, rows, LANES), F32),
                pltpu.VMEM((2 * rows, depth), F32),
            ],
        ),
        out_shape=[
            jax.ShapeDtypeStruct((2 * rows, count), BF16),
            jax.ShapeDtypeStruct((rows, depth), F32),
            jax.ShapeDtypeStruct((rows, depth), F32),
        ],
        compiler_params=params(48),
        name="score_grad",
    )(bit, e, low_p, pairing, *tparts, *rparts, *cparts)


def proto_kernel(order_ref, low_ref, keep_in, send_in, keep_ref, send_ref, low_t):
    @pl.when(pl.program_id(0) == 0)
    def _():
        low_t[...] = low_ref[...].astype(F32).T.astype(BF16)

    keep_ref[0] = jnp.dot(low_t[...], keep_in[...], preferred_element_type=F32)
    send_ref[0] = jnp.dot(low_t[...], send_in[...], preferred_element_type=F32)


def proto_grad(order, low, ds, width):
    rows, depth = low.shape
    half = order.shape[0] // 2
    block = pl.BlockSpec((1, depth, width), lambda k, o: (k, 0, 0))
    return pl.pallas_call(
        proto_kernel,
        grid_spec=pltpu.PrefetchScalarGridSpec(
            num_scalar_prefetch=1,
            grid=(half,),
            in_specs=[
                whole(low.shape),
                pl.BlockSpec((rows, width), lambda k, o: (0, o[k])),
                pl.BlockSpec((rows, width), lambda k, o: (0, o[half + k])),
            ],
            out_specs=[block, block],
            scratch_shapes=[pltpu.VMEM((depth, rows), BF16)],
        ),
        out_shape=[jax.ShapeDtypeStruct((half, depth, width), F32)] * 2,
        compiler_params=params(24),
        name="proto_grad",
    )(order, low, ds, ds)


def finish_proto_kernel(m, order_ref, *refs):
    pieces, p_ref, out_ref = refs[:m], refs[m], refs[-1]
    xf = p_ref[...].astype(F32)
    inv = inverse_norm(xf)
    unit = xf * inv
    for i in range(m):

        @pl.when(pl.program_id(0) == i)
        def _(i=i):
            g = pieces[i][0].T
            out_ref[...] = inv * (g - unit * jnp.sum(unit * g, -1, keepdims=True))


def finish_proto(order, pieces, protos, out=None):
    m = len(pieces)
    depth, width = pieces[0].shape[1:]
    block = pl.BlockSpec((width, depth), lambda k, o: (o[k], 0))
    more = () if out is None else (out,)
    return pl.pallas_call(
        functools.partial(finish_proto_kernel, m),
        grid_spec=pltpu.PrefetchScalarGridSpec(
            num_scalar_prefetch=1,
            grid=(m,),
            in_specs=[whole((1, depth, width))] * m
            + [block]
            + [pl.BlockSpec(memory_space=pl.ANY)] * len(more),
            out_specs=block,
        ),
        out_shape=jax.ShapeDtypeStruct(protos.shape, F32),
        input_output_aliases={m + 2: 0} if more else {},
        compiler_params=params(24),
        name="finish_proto",
    )(order, *pieces, protos, *more)


def finish_view_kernel(bit_ref, keep_ref, other_ref, one_ref, two_ref, g_one, g_two):
    def put(x_ref, grad_ref, out_ref):
        xf = x_ref[...].astype(F32)
        inv = inverse_norm(xf)
        unit = xf * inv
        g = grad_ref[...]
        out_ref[...] = inv * (g - unit * jnp.sum(unit * g, -1, keepdims=True))

    @pl.when(bit_ref[0] == 0)
    def _():
        put(one_ref, keep_ref, g_one)
        put(two_ref, other_ref, g_two)

    @pl.when(bit_ref[0] != 0)
    def _():
        put(one_ref, other_ref, g_one)
        put(two_ref, keep_ref, g_two)


def finish_views(bit, keep, other, one, two):
    rows, depth = one.shape
    step = min(rows, 256)
    block = pl.BlockSpec((step, depth), lambda k, b: (k, 0))
    return pl.pallas_call(
        finish_view_kernel,
        grid_spec=pltpu.PrefetchScalarGridSpec(
            num_scalar_prefetch=1,
            grid=(rows // step,),
            in_specs=[block] * 4,
            out_specs=[block] * 2,
        ),
        out_shape=[jax.ShapeDtypeStruct((rows, depth), F32)] * 2,
        compiler_params=params(24),
        name="finish_views",
    )(bit, keep, other, one, two)


def swap(x, axes, n, mask):
    return lax.ppermute(x, axes, [(i, i ^ mask) for i in range(n)])


def sum_parts(x, axes, first):
    n = lax.axis_size(axes)
    bits = n.bit_length() - 1
    groups, at = ([(0, first)], first) if first else ([], 0)
    while at < bits:
        groups.append((at, min(2, bits - at)))
        at += 2
    parts = [x]
    for low, size in groups:
        x = sum(parts[1:], parts[0])
        parts = [x] + [swap(x, axes, n, m << low) for m in range(1, 1 << size)]
    return parts


def position_masks(bits):
    n = 1 << len(bits)
    return [
        sum(((i >> (len(bits) - 1 - j)) & 1) << b for j, b in enumerate(bits)) for i in range(n)
    ]


def scatter_stream(keep, send, n, bits):
    for j, b in enumerate(bits):
        recv = swap(send, SEG_AXES, n, 1 << b)
        half = keep.shape[0] // 2
        if half:
            send = keep[half:] + recv[half:]
            keep = keep[:half] + recv[:half]
        else:
            keep = keep + recv
    return keep


def per_device(view_one, view_two, prototypes, pairing):
    rows, depth = view_one.shape
    count = prototypes.shape[0]
    n = lax.axis_size(SEG_AXES)
    nz = lax.axis_size("proto")
    me = lax.axis_index(SEG_AXES).astype(jnp.int32)
    zbit = (lax.axis_index("proto") & 1).astype(jnp.int32).reshape(1)

    width = min(count, 512)
    e, low_p, low, c, t = front(pairing, view_one, view_two, prototypes, width)

    cparts = sum_parts(c, SEG_AXES, 1)
    tparts = rparts = sum_parts(row_pass(e, cparts, (t,)), "proto", 0)
    for _ in range(ITERS - 1):
        cparts = sum_parts(col_pass(e, rparts), SEG_AXES, 1)
        rparts = sum_parts(row_pass(e, cparts), "proto", 0)

    ds, keep_v, send_v = score_grad(zbit, e, low_p, pairing, tparts, rparts, cparts, width)

    keep_v = keep_v + swap(send_v, "proto", nz, 1)
    b = 2
    while b < nz:
        keep_v = keep_v + swap(keep_v, "proto", nz, b)
        b *= 2
    other_v = swap(keep_v, "proto", nz, 1)
    grad_one, grad_two = finish_views(zbit, keep_v, other_v, view_one, view_two)

    nbits = n.bit_length() - 1
    streams = max(1, min(2, count // (n * LANES)))
    block = count // (n * streams)
    orders = [[0] + list(range(1, nbits)), [0] + list(range(nbits - 1, 0, -1))][:streams]
    shares = []
    for s, bits in enumerate(orders):
        masks = jnp.array(position_masks(bits), jnp.int32)
        order = (masks ^ me) + s * n
        keep, send = proto_grad(order, low, ds, block)
        shares.append(scatter_stream(keep, send, n, bits))

    groups = [[], []]
    for s, bits in enumerate(orders):
        held = {0: shares[s]}
        for b in reversed(bits):
            fresh = {m ^ (1 << b): swap(x, SEG_AXES, n, 1 << b) for m, x in held.items()}
            if b == bits[0]:
                groups[0] += [(m, s, x) for m, x in held.items()]
                groups[1] += [(m, s, x) for m, x in fresh.items()]
            held.update(fresh)
    out = None
    for group in groups:
        order = jnp.stack([(me ^ m) + s * n for m, s, _ in group])
        out = finish_proto(order, [x for _, _, x in group], prototypes, out)
    return grad_one, grad_two, out


def solution(mesh):
    placed = (
        P(("batch", "replica"), None),
        P(("batch", "replica"), None),
        P("proto", None),
        P(("batch", "replica"), None),
    )
    return jax.shard_map(
        per_device,
        mesh=mesh,
        in_specs=placed,
        out_specs=(P(("batch", "replica"), None), P(("batch", "replica"), None), P("proto", None)),
        check_vma=False,
    )
```

```python
import functools

import jax
import jax.numpy as jnp
from jax import lax
from jax.experimental import pallas as pl
from jax.experimental.pallas import tpu as pltpu
from jax.sharding import PartitionSpec as P


ITERS = 3
SEG_AXES = ("batch", "replica")
F32 = jnp.float32
BF16 = jnp.bfloat16

softness_divisor = 0.1
LANES = 128


def params(limit_mib, axes=1):
    return pltpu.CompilerParams(
        vmem_limit_bytes=limit_mib << 20, dimension_semantics=("arbitrary",) * axes or None
    )


def whole(shape):
    return pl.BlockSpec(shape, lambda *_: (0,) * len(shape))


def inverse_norm(xf):
    return lax.rsqrt(jnp.sum(xf * xf, -1, keepdims=True) + 1e-06)


def unit_low(x):
    xf = x.astype(F32)
    return (xf * inverse_norm(xf)).astype(BF16)


def lane_fold(x):
    return sum(x[:, i : i + LANES] for i in range(0, x.shape[1], LANES))


def row_fold(x):
    return sum(x[i : i + 8] for i in range(0, x.shape[0], 8))


def to_row(acc):
    return jnp.sum(acc.T, axis=0, keepdims=True)


def to_column(row):
    return jnp.broadcast_to(row, (LANES, row.shape[1])).T


def total(refs, lo, hi):
    return sum(r[lo:hi, :] for r in refs)


def front_kernel(pair_ref, one_ref, two_ref, p_ref, e_ref, lowp_ref, low_ref, c_ref, t_ref, tacc):
    k = pl.program_id(0)
    rows = one_ref.shape[0]

    @pl.when(k == 0)
    def _():
        low_ref[:rows] = unit_low(one_ref[...])
        low_two = unit_low(two_ref[...])
        spread = (lax.broadcasted_iota(jnp.int32, (rows, rows), 0) == pair_ref[...]).astype(F32)
        low_ref[rows:] = jnp.dot(
            spread.T.astype(BF16), low_two, preferred_element_type=F32
        ).astype(BF16)
        tacc[...] = jnp.zeros_like(tacc)

    low_p = unit_low(p_ref[...])
    lowp_ref[...] = low_p
    step = min(rows, 64)
    for v in range(2):
        s = lax.dot_general(
            low_ref[v * rows : (v + 1) * rows],
            low_p,
            (((1,), (1,)), ((), ())),
            preferred_element_type=F32,
        )
        cacc = jnp.zeros((8, s.shape[1]), F32)
        for i in range(0, rows, step):
            e = jnp.exp(s[i : i + step] * (1.0 / softness_divisor))
            e_ref[v, i : i + step, :] = e
            tacc[v, i : i + step] += lane_fold(e)
            cacc = cacc + row_fold(e * e)
        c_ref[v : v + 1, :] = jnp.sum(cacc, axis=0, keepdims=True)

    @pl.when(k == pl.num_programs(0) - 1)
    def _():
        for v in range(2):
            t_ref[v : v + 1, :] = to_row(tacc[v])


def in_hbm(x):
    return pltpu.with_memory_space_constraint(x, pltpu.HBM)


def in_vmem(x):
    return pltpu.with_memory_space_constraint(x, pltpu.VMEM)


RESIDENT = pl.BlockSpec(memory_space=pltpu.VMEM)
SCALARS = pl.BlockSpec(memory_space=pltpu.SMEM)


def front(pairing, one, two, protos, width):
    rows, depth = one.shape
    count = protos.shape[0]
    return pl.pallas_call(
        front_kernel,
        grid=(count // width,),
        in_specs=[
            whole(pairing.shape),
            whole(one.shape),
            whole(two.shape),
            pl.BlockSpec((width, depth), lambda k: (k, 0)),
        ],
        out_specs=[
            pl.BlockSpec((2, rows, width), lambda k: (0, 0, k)),
            pl.BlockSpec((width, depth), lambda k: (k, 0)),
            whole((2 * rows, depth)),
            pl.BlockSpec((2, width), lambda k: (0, k)),
            whole((2, rows)),
        ],
        out_shape=[
            pltpu.VMEM((2, rows, count), F32),
            pltpu.VMEM((count, depth), BF16),
            pltpu.VMEM((2 * rows, depth), BF16),
            jax.ShapeDtypeStruct((2, count), F32),
            jax.ShapeDtypeStruct((2, rows), F32),
        ],
        scratch_shapes=[pltpu.VMEM((2, rows, LANES), F32)],
        compiler_params=params(24),
        name="front",
    )(*[in_hbm(x) for x in (pairing, one, two, protos)])


def row_kernel(n, e_ref, *refs):
    cparts, rest = refs[:n], refs[n:]
    t_refs, (out_ref, vb, acc) = rest[:-3], rest[-3:]
    rows, count = e_ref.shape[1:]
    step = min(rows, 64)
    v = 1.0 / total(cparts, 0, 2)
    for i in range(2):
        vb[i] = jnp.broadcast_to(v[i : i + 1], (8, count))

    def body(k, _):
        at = pl.ds(pl.multiple_of(k * step, step), step)
        for i in range(2):
            a = jnp.zeros((step, LANES), F32)
            for j in range(0, count, LANES):
                e = e_ref[i, at, j : j + LANES]
                scale = jnp.concatenate([vb[i, :, j : j + LANES]] * (step // 8), axis=0)
                a = a + e * e * scale
            acc[i, at, :] = a
        return 0

    lax.fori_loop(0, rows // step, body, 0)
    for i in range(2):
        out_ref[i : i + 1, :] = to_row(acc[i])
    for t_ref in t_refs:
        out_ref[2:4, :] = t_ref[...]


def row_pass(e, cparts, extra=()):
    _, rows, count = e.shape
    height = 2 + 2 * len(extra)
    return pl.pallas_call(
        functools.partial(row_kernel, len(cparts)),
        in_specs=[RESIDENT] * (1 + len(cparts) + len(extra)),
        out_shape=jax.ShapeDtypeStruct((height, rows), F32),
        scratch_shapes=[pltpu.VMEM((2, 8, count), F32), pltpu.VMEM((2, rows, LANES), F32)],
        compiler_params=params(8, 0),
        name="row_pass",
    )(in_vmem(e), *cparts, *extra)


def col_kernel(n, e_ref, *refs):
    rparts, (out_ref, ub, acc) = refs[:n], refs[n:]
    rows, count = e_ref.shape[1:]
    step = min(rows, 64)
    u = 1.0 / total(rparts, 0, 2)
    for i in range(2):
        ub[i] = to_column(u[i : i + 1])
    acc[...] = jnp.zeros_like(acc)

    def body(k, _):
        at = pl.ds(pl.multiple_of(k * step, step), step)
        for i in range(2):
            u = ub[i, at, :]
            for j in range(0, count, LANES):
                e = e_ref[i, at, j : j + LANES]
                acc[i, :, j : j + LANES] += row_fold(e * e * u)
        return 0

    lax.fori_loop(0, rows // step, body, 0)
    for i in range(2):
        out_ref[i : i + 1, :] = jnp.sum(acc[i], axis=0, keepdims=True)


def col_pass(e, rparts):
    _, rows, count = e.shape
    return pl.pallas_call(
        functools.partial(col_kernel, len(rparts)),
        in_specs=[RESIDENT] * (1 + len(rparts)),
        out_shape=jax.ShapeDtypeStruct((2, count), F32),
        scratch_shapes=[pltpu.VMEM((2, rows, LANES), F32), pltpu.VMEM((2, 8, count), F32)],
        compiler_params=params(8, 0),
        name="col_pass",
    )(in_vmem(e), *rparts)


def score_kernel(nr, nc, bit_ref, e_ref, lowp_ref, pair_ref, *refs):
    tparts, rparts, cparts = refs[:nr], refs[nr : 2 * nr], refs[2 * nr : 2 * nr + nc]
    ds_ref, keep_ref, send_ref, ub, wb, vb, even, odd, acc = refs[2 * nr + nc :]
    rows, count = e_ref.shape[1:]
    width = even.shape[1]
    blocks = count // width
    gain = 0.5 / softness_divisor

    u = gain / total(rparts, 0, 2)
    w = gain / total(tparts, 2, 4)
    v = 1.0 / total(cparts, 0, 2)
    for i in range(2):
        ub[i] = to_column(u[i : i + 1])
        wb[i] = to_column(w[i : i + 1])
        vb[i] = jnp.broadcast_to(v[i : i + 1], (8, count))
    acc[...] = jnp.zeros_like(acc)
    step = min(rows, 32)

    def fill(k, buf):
        for j in range(0, width, LANES):
            lanes = pl.ds(pl.multiple_of(k * width + j, LANES), LANES)
            v_one = jnp.concatenate([vb[0, :, lanes]] * (step // 8), axis=0)
            v_two = jnp.concatenate([vb[1, :, lanes]] * (step // 8), axis=0)
            for i in range(0, rows, step):
                e_one, e_two = e_ref[0, i : i + step, lanes], e_ref[1, i : i + step, lanes]
                u_one, u_two = ub[0, i : i + step], ub[1, i : i + step]
                w_one, w_two = wb[0, i : i + step], wb[1, i : i + step]
                d_one = (e_one * w_one - e_two * e_two * u_two * v_two).astype(BF16)
                d_two = (e_two * w_two - e_one * e_one * u_one * v_one).astype(BF16)
                buf[i : i + step, j : j + LANES] = d_one
                buf[rows + i : rows + i + step, j : j + LANES] = d_two
                ds_ref[i : i + step, lanes] = d_one
                ds_ref[rows + i : rows + i + step, lanes] = d_two

    def use(k, buf):
        low_p = lowp_ref[pl.ds(pl.multiple_of(k * width, width), width), :]
        acc[...] += jnp.dot(buf[...], low_p, preferred_element_type=F32)

    fill(0, even)

    def body(h, _):
        use(2 * h, even)
        fill(2 * h + 1, odd)
        use(2 * h + 1, odd)
        fill(jnp.minimum(2 * h + 2, blocks - 2), even)
        return 0

    lax.fori_loop(0, blocks // 2, body, 0)

    spread = (lax.broadcasted_iota(jnp.int32, (rows, rows), 0) == pair_ref[...]).astype(F32)
    d_two = jnp.dot(
        spread, acc[rows:], preferred_element_type=F32, precision=lax.Precision.HIGHEST
    )

    @pl.when(bit_ref[0] == 0)
    def _():
        keep_ref[...] = acc[:rows]
        send_ref[...] = d_two

    @pl.when(bit_ref[0] != 0)
    def _():
        keep_ref[...] = d_two
        send_ref[...] = acc[:rows]


def score_grad(bit, e, low_p, pairing, tparts, rparts, cparts, width):
    _, rows, count = e.shape
    depth = low_p.shape[1]
    return pl.pallas_call(
        functools.partial(score_kernel, len(rparts), len(cparts)),
        in_specs=[SCALARS] + [RESIDENT] * (3 + len(tparts) + len(rparts) + len(cparts)),
        out_shape=[
            pltpu.VMEM((2 * rows, count), BF16),
            jax.ShapeDtypeStruct((rows, depth), F32),
            jax.ShapeDtypeStruct((rows, depth), F32),
        ],
        scratch_shapes=[
            pltpu.VMEM((2, rows, LANES), F32),
            pltpu.VMEM((2, rows, LANES), F32),
            pltpu.VMEM((2, 8, count), F32),
            pltpu.VMEM((2 * rows, width), BF16),
            pltpu.VMEM((2 * rows, width), BF16),
            pltpu.VMEM((2 * rows, depth), F32),
        ],
        compiler_params=params(16, 0),
        name="score_grad",
    )(bit, in_vmem(e), in_vmem(low_p), pairing, *tparts, *rparts, *cparts)


def proto_kernel(order_ref, low_ref, ds_ref, keep_ref, send_ref, low_t):
    half, _, width = keep_ref.shape
    low_t[...] = low_ref[...].astype(F32).T.astype(BF16)

    def body(g, _):
        for out, at in ((send_ref, half + g), (keep_ref, g)):
            lanes = pl.ds(pl.multiple_of(order_ref[at] * width, width), width)
            out[g] = jnp.dot(low_t[...], ds_ref[:, lanes], preferred_element_type=F32)
        return 0

    lax.fori_loop(0, half, body, 0)


def proto_grad(order, low, ds, width):
    rows, depth = low.shape
    half = order.shape[0] // 2
    return pl.pallas_call(
        proto_kernel,
        in_specs=[SCALARS, RESIDENT, RESIDENT],
        out_shape=[pltpu.VMEM((half, depth, width), F32)] * 2,
        scratch_shapes=[pltpu.VMEM((depth, rows), BF16)],
        compiler_params=params(16, 0),
        name="proto_grad",
    )(order, in_vmem(low), in_vmem(ds))


def unit_back(grad, x):
    xf = x.astype(F32)
    inv = inverse_norm(xf)
    unit = xf * inv
    return inv * (grad - unit * jnp.sum(unit * grad, -1, keepdims=True))


def share_kernel(at_ref, keep_ref, recv_ref, p_ref, out_ref):
    out_ref[...] = unit_back((keep_ref[0] + recv_ref[0]).T, p_ref[...])


def finish_share(at, keep, recv, protos):
    _, depth, width = keep.shape
    return pl.pallas_call(
        share_kernel,
        grid_spec=pltpu.PrefetchScalarGridSpec(
            num_scalar_prefetch=1,
            grid=(1,),
            in_specs=[whole(keep.shape)] * 2
            + [pl.BlockSpec((width, depth), lambda k, a: (a[0], 0))],
            out_specs=whole((width, depth)),
        ),
        out_shape=jax.ShapeDtypeStruct((width, depth), F32),
        compiler_params=params(8),
        name="finish_share",
    )(at, keep, recv, in_hbm(protos))


def place_kernel(m, order_ref, *refs):
    pieces, out_ref, sems = refs[:m], refs[-2], refs[-1]
    width = pieces[0].shape[0]
    copies = []
    for i in range(m):
        rows = pl.ds(pl.multiple_of(order_ref[i] * width, width), width)
        copies.append(pltpu.make_async_copy(pieces[i], out_ref.at[rows, :], sems.at[i]))
        copies[-1].start()
    for copy in copies:
        copy.wait()


def place(order, pieces, shape, out=None):
    m = len(pieces)
    more = () if out is None else (out,)
    return pl.pallas_call(
        functools.partial(place_kernel, m),
        in_specs=[SCALARS]
        + [RESIDENT] * m
        + [pl.BlockSpec(memory_space=pl.ANY)] * len(more),
        out_specs=pl.BlockSpec(memory_space=pltpu.HBM),
        out_shape=jax.ShapeDtypeStruct(shape, F32),
        input_output_aliases={m + 1: 0} if more else {},
        scratch_shapes=[pltpu.SemaphoreType.DMA((m,))],
        compiler_params=params(8, 0),
        name="place",
    )(order, *[in_vmem(x) for x in pieces], *more)


def finish_view_kernel(bit_ref, keep_ref, other_ref, one_ref, two_ref, g_one, g_two):
    @pl.when(bit_ref[0] == 0)
    def _():
        g_one[...] = unit_back(keep_ref[...], one_ref[...])
        g_two[...] = unit_back(other_ref[...], two_ref[...])

    @pl.when(bit_ref[0] != 0)
    def _():
        g_one[...] = unit_back(other_ref[...], one_ref[...])
        g_two[...] = unit_back(keep_ref[...], two_ref[...])


def finish_views(bit, keep, other, one, two):
    rows, depth = one.shape
    step = min(rows, 128)
    block = pl.BlockSpec((step, depth), lambda k, b: (k, 0))
    return pl.pallas_call(
        finish_view_kernel,
        grid_spec=pltpu.PrefetchScalarGridSpec(
            num_scalar_prefetch=1,
            grid=(rows // step,),
            in_specs=[block] * 4,
            out_specs=[block] * 2,
        ),
        out_shape=[jax.ShapeDtypeStruct((rows, depth), F32)] * 2,
        compiler_params=params(16),
        name="finish_views",
    )(bit, keep, other, in_hbm(one), in_hbm(two))


def swap(x, axes, n, mask):
    return lax.ppermute(x, axes, [(i, i ^ mask) for i in range(n)])


def sum_parts(x, axes, first):
    n = lax.axis_size(axes)
    bits = n.bit_length() - 1
    groups, at = ([(0, first)], first) if first else ([], 0)
    while at < bits:
        groups.append((at, min(2, bits - at)))
        at += 2
    parts = [x]
    for low, size in groups:
        x = sum(parts[1:], parts[0])
        parts = [x] + [swap(x, axes, n, m << low) for m in range(1, 1 << size)]
    return parts


def position_masks(bits):
    n = 1 << len(bits)
    return [
        sum(((i >> (len(bits) - 1 - j)) & 1) << b for j, b in enumerate(bits)) for i in range(n)
    ]


def scatter_stream(keep, send, n, bits):
    for b in bits:
        recv = swap(send, SEG_AXES, n, 1 << b)
        half = keep.shape[0] // 2
        if half:
            send = keep[half:] + recv[half:]
            keep = keep[:half] + recv[:half]
    return keep, recv


def per_device(view_one, view_two, prototypes, pairing):
    count = prototypes.shape[0]
    n = lax.axis_size(SEG_AXES)
    nz = lax.axis_size("proto")
    me = lax.axis_index(SEG_AXES).astype(jnp.int32)
    zbit = (lax.axis_index("proto") & 1).astype(jnp.int32).reshape(1)

    nbits = n.bit_length() - 1
    streams = max(1, min(2, count // (n * LANES)))
    block = count // (n * streams)
    bit_orders = [[0] + list(range(1, nbits)), [0] + list(range(nbits - 1, 0, -1))][:streams]
    tables = [
        (jnp.array(position_masks(bits), jnp.int32) ^ me) + s * n
        for s, bits in enumerate(bit_orders)
    ]
    pairing, zbit, tables = lax.optimization_barrier((pairing, zbit, tables))

    width = min(count, 512)
    e, low_p, low, c, t = front(pairing, view_one, view_two, prototypes, width)

    cparts = sum_parts(c, SEG_AXES, 1)
    tparts = rparts = sum_parts(row_pass(e, cparts, (t,)), "proto", 0)
    for _ in range(ITERS - 1):
        cparts = sum_parts(col_pass(e, rparts), SEG_AXES, 1)
        rparts = sum_parts(row_pass(e, cparts), "proto", 0)

    ds, keep_v, send_v = score_grad(zbit, e, low_p, pairing, tparts, rparts, cparts, width)

    recv = swap(send_v, "proto", nz, 1)
    keep_v = keep_v + recv
    b = 2
    while b < nz:
        recv = swap(keep_v, "proto", nz, b)
        keep_v = keep_v + recv
        b *= 2
    other_v = swap(keep_v, "proto", nz, 1)

    shares = []
    for s, bits in enumerate(bit_orders):
        keep, send = proto_grad(tables[s], low, ds, block)
        keep, recv = scatter_stream(keep, send, n, bits)
        shares.append(finish_share(tables[s][:1], keep, recv, prototypes))

    near, far = [], []
    held = [{0: x} for x in shares]
    for j in range(nbits - 1, -1, -1):
        for s, bits in enumerate(bit_orders):
            fresh = {}
            for m, x in held[s].items():
                fresh[m ^ (1 << bits[j])] = swap(x, SEG_AXES, n, 1 << bits[j])
            if j == 0:
                near += [(m, s, x) for m, x in held[s].items()]
                far += [(m, s, x) for m, x in fresh.items()]
            held[s].update(fresh)
    masks = [position_masks(bits) for bits in bit_orders]
    out = None
    for group in (near, far):
        order = jnp.stack([tables[s][masks[s].index(m)] for m, s, _ in group])
        out = place(order, [x for _, _, x in group], prototypes.shape, out)
    grad_one, grad_two = finish_views(zbit, keep_v, other_v, view_one, view_two)
    return grad_one, grad_two, out


def solution(mesh):
    placed = (
        P(("batch", "replica"), None),
        P(("batch", "replica"), None),
        P("proto", None),
        P(("batch", "replica"), None),
    )

    return jax.shard_map(
        per_device,
        mesh=mesh,
        in_specs=placed,
        out_specs=(P(("batch", "replica"), None), P(("batch", "replica"), None), P("proto", None)),
        check_vma=False,
    )
```
